256 devices in a mesh: stream: 16 (over y_lo, z), azim: 4 (over x), slab: 4 (over y_hi, core).
Axes of the slice: x: 4, y: 4 (y_hi: 2, y_lo: 2; y = y_hi * 2 + y_lo), z: 8, core: 2. Of those that a mesh axis runs over, the one named last changes fastest.
Arguments:
- field: bfloat16 [8, 8, 4096, 256], P('azim', 'slab', 'stream'), may hold values from -6 to 6
- gain_stream: float32 [256], replicated, may hold values from 0.5 to 1.5
- gain_cross: float32 [256], replicated, may hold values from 0.5 to 1.5
- stream_query: bfloat16 [256, 256], replicated, may hold values from -0.375 to 0.375
- stream_key: bfloat16 [256, 256], replicated, may hold values from -0.375 to 0.375
- stream_value: bfloat16 [256, 256], replicated, may hold values from -0.375 to 0.375
- stream_out: bfloat16 [256, 256], replicated, may hold values from -0.375 to 0.375
- cross_query: bfloat16 [256, 256], replicated, may hold values from -0.375 to 0.375
- cross_key: bfloat16 [256, 256], replicated, may hold values from -0.375 to 0.375
- cross_value: bfloat16 [256, 256], replicated, may hold values from -0.375 to 0.375
- cross_out: bfloat16 [256, 256], replicated, may hold values from -0.375 to 0.375
- stream_scale: float32 [4], replicated, may hold values from 10 to 30
- cross_scale: float32 [4], replicated, may hold values from 10 to 30
- azim_bias: float32 [4, 8], replicated, may hold values from -3 to 3
- azim_order: int32 [8], replicated, may hold values from 0 to 7, each once
- block_lists: int32 [32, 4], P('stream'), may hold values from 0 to 31, as said below
Outputs:
- layer_out: bfloat16 [8, 8, 4096, 256], P('azim', 'slab', 'stream')
The draws below stay inside these ranges and needn't reach their ends.
Inputs may be any that keep to these rules, and one draw needn't show every extreme that they name: `block_lists`: blocks are numbered along the line, 2 to a device in order. Each entry of row b is block c of the device e steps away, along the closed streamwise loop, from the device of block b, with |e| <= 2 and 0 <= c < 2; the blocks named in a row are distinct. `azim_order`: A permutation of the 8 azimuthal positions.
All inputs are finite; a program needn't handle non-finite values.
Results may differ from the reference program's by a relative error of at most 0.011.
Values may be sent and summed in bfloat16 or wider, within the bound.
No kernel may reach another device: no remote copies, remote signals or barrier semaphores. Data moves between devices by JAX's collectives and lax.ppermute only.
A program may use at most 64 MiB of HBM per device.

```python
import math
import jax
import jax.numpy as jnp
from jax import lax

D = 256
HEADS = 4
HEAD_DIM = 64
BLOCK = 128
REACH = 2
LIST_LEN = 4
BLOCKS_DEV = 2
NS = 4096
NA = 8
NR = 8
BLOCKS = 32


def draw_block_lists(key, part):
    cycle_size = BLOCKS // BLOCKS_DEV
    reach_count = min(2 * REACH + 1, cycle_size)
    window = reach_count * BLOCKS_DEV
    start_shift = REACH if cycle_size >= 2 * REACH + 1 else 0
    row_keys = jax.random.split(key, BLOCKS)

    def choose(row_key):
        return jax.random.permutation(row_key, window)[:LIST_LEN]
    picked = jax.vmap(choose)(row_keys).astype(jnp.int32)
    blocks = jnp.arange(BLOCKS, dtype=jnp.int32)[:, None]
    device = blocks // BLOCKS_DEV
    offset = picked // BLOCKS_DEV - start_shift
    within = picked % BLOCKS_DEV
    return ((device + offset) % cycle_size * BLOCKS_DEV + within).astype(jnp.int32)


def steps_of(key, extent, shards, low, high):
    loudness = 1.0
    for axis_at, parts in shards:
        draws = jax.random.uniform(jax.random.fold_in(jax.random.fold_in(key, 6), axis_at), (parts,), jnp.float32, low / len(shards), high / len(shards))
        loudness = loudness * jnp.repeat(jnp.exp(draws), extent[axis_at] // parts).reshape((-1,) + (1,) * (len(extent) - 1 - axis_at))
    return loudness


def normal_values(key, dims, deviation, most, pieces=(), kind=jnp.bfloat16):
    array = jax.random.normal(key, dims, jnp.float32) * deviation
    if len(pieces) > 0:
        array = steps_of(key, dims, pieces, -0.22, 0.18) * array
    return jnp.clip(array, min=-most, max=most).astype(kind)


def setup_inputs(seed: int = 0) -> dict:
    arg_keys = jax.random.split(jax.random.key(seed), 17)
    field = normal_values(arg_keys[0], (NA, NR, NS, D), 1.0, 6.0, ((0, 4), (1, 4), (2, 16)))
    gain_stream = jnp.clip(1.0 + 0.1 * jax.random.normal(arg_keys[1], (D,), jnp.float32), 0.5, 1.5)
    gain_cross = jnp.clip(1.0 + 0.1 * jax.random.normal(arg_keys[2], (D,), jnp.float32), 0.5, 1.5)
    stream_query = normal_values(arg_keys[3], (D, D), D ** -0.5, 0.375)
    stream_key = normal_values(arg_keys[4], (D, D), D ** -0.5, 0.375)
    stream_value = normal_values(arg_keys[5], (D, D), D ** -0.5, 0.375)
    stream_out = normal_values(arg_keys[6], (D, D), D ** -0.5, 0.375)
    cross_query = normal_values(arg_keys[7], (D, D), D ** -0.5, 0.375)
    cross_key = normal_values(arg_keys[8], (D, D), D ** -0.5, 0.375)
    cross_value = normal_values(arg_keys[9], (D, D), D ** -0.5, 0.375)
    cross_out = normal_values(arg_keys[10], (D, D), D ** -0.5, 0.375)
    stream_scale = jnp.clip(jnp.exp(jax.random.uniform(arg_keys[11], (HEADS,), jnp.float32, math.log(10.0), math.log(30.0))), 10.0, 30.0)
    cross_scale = jnp.clip(jnp.exp(jax.random.uniform(arg_keys[12], (HEADS,), jnp.float32, math.log(10.0), math.log(30.0))), 10.0, 30.0)
    azim_bias = normal_values(arg_keys[13], (HEADS, NA), 1.0, 3.0, (), jnp.float32)
    azim_order = jax.random.permutation(arg_keys[14], NA).astype(jnp.int32)
    block_lists = draw_block_lists(jax.random.fold_in(arg_keys[16], 71), 0)
    return {"field": field, "gain_stream": gain_stream, "gain_cross": gain_cross, "stream_query": stream_query, "stream_key": stream_key, "stream_value": stream_value, "stream_out": stream_out, "cross_query": cross_query, "cross_key": cross_key, "cross_value": cross_value, "cross_out": cross_out, "stream_scale": stream_scale, "cross_scale": cross_scale, "azim_bias": azim_bias, "azim_order": azim_order, "block_lists": block_lists}


def norm_rows(values, gain_row):
    floats = values.astype(jnp.float32)
    scaled = floats * lax.rsqrt(lax.optimization_barrier(jnp.mean(floats * floats, axis=-1, keepdims=True)) + 1e-05)
    return (scaled * gain_row).astype(jnp.bfloat16)

def project(row_block, weight):
    flattened = row_block.reshape(-1, row_block.shape[-1])
    product = jnp.dot(flattened, weight, preferred_element_type=jnp.float32)
    return product.reshape(row_block.shape[:-1] + (weight.shape[1],))

def head_unit(values, scales):
    shaped = values.reshape(values.shape[:-1] + (HEADS, HEAD_DIM))
    shaped = shaped * lax.rsqrt(lax.optimization_barrier(jnp.mean(shaped * shaped, axis=-1, keepdims=True)) + 1e-06)
    if scales is not None:
        shaped = shaped * (scales / HEAD_DIM)[:, None]
    return shaped.reshape(values.shape).astype(jnp.bfloat16)

def section_bias(azim_bias, azim_order, radials):
    azimuths = azim_order.shape[0]
    distance = (azim_order[:, None] - azim_order[None, :]) % azimuths
    onehot = (distance[:, :, None] == jnp.arange(azimuths, dtype=jnp.int32)[None, None, :]).astype(jnp.float32)
    lookup = jnp.einsum('abm,hm->hab', onehot, azim_bias.astype(jnp.float32), precision=lax.Precision.HIGHEST)
    lookup = jnp.broadcast_to(lookup[:, :, None, :, None], (HEADS, azimuths, radials, azimuths, radials))
    return lookup.reshape(HEADS, azimuths * radials, azimuths * radials)

def lowered(weights):
    rounded = lax.optimization_barrier(weights.astype(jnp.bfloat16))
    return rounded.astype(jnp.float32)

def reference(field, gain_stream, gain_cross, stream_query, stream_key, stream_value, stream_out, cross_query, cross_key, cross_value, cross_out, stream_scale, cross_scale, azim_bias, azim_order, block_lists):
    azimuths, radials, stream_len, width = field.shape
    line_count = azimuths * radials
    tokens = field.reshape(line_count, stream_len, width)
    normed = norm_rows(tokens, gain_stream)
    queries = head_unit(project(normed, stream_query), stream_scale)
    keys = head_unit(project(normed, stream_key), None)
    values = project(normed, stream_value).astype(jnp.bfloat16)
    key_blocks = keys.reshape(line_count, BLOCKS, BLOCK, width)
    value_blocks = values.reshape(line_count, BLOCKS, BLOCK, width)

    def one_block(inputs):
        index, listed = inputs
        query_part = lax.dynamic_slice_in_dim(queries, index * BLOCK, BLOCK, 1)
        query_part = query_part.reshape(line_count, BLOCK, HEADS, HEAD_DIM).astype(jnp.float32)
        picked_keys = jnp.take(key_blocks, listed, axis=1).reshape(line_count, LIST_LEN * BLOCK, HEADS, HEAD_DIM).astype(jnp.float32)
        picked_values = jnp.take(value_blocks, listed, axis=1).reshape(line_count, LIST_LEN * BLOCK, HEADS, HEAD_DIM).astype(jnp.float32)
        scores = jnp.einsum('lqhd,lkhd->lhqk', query_part, picked_keys)
        weights = jnp.exp(scores)
        totals = lax.optimization_barrier(jnp.sum(weights, axis=-1))
        weighted = jnp.einsum('lhqk,lkhd->lqhd', lowered(weights), picked_values)
        attended = weighted / jnp.transpose(totals, (0, 2, 1))[..., None]
        return attended.reshape(line_count, BLOCK, width).astype(jnp.bfloat16)
    attended = lax.map(one_block, (jnp.arange(BLOCKS, dtype=jnp.int32), block_lists))
    attended = jnp.transpose(attended, (1, 0, 2, 3)).reshape(line_count, stream_len, width)
    after_stream = (tokens.astype(jnp.float32) + project(attended, stream_out)).astype(jnp.bfloat16)
    normed_cross = norm_rows(after_stream, gain_cross)
    cross_queries = head_unit(project(normed_cross, cross_query), cross_scale)
    cross_keys = head_unit(project(normed_cross, cross_key), None)
    cross_values = project(normed_cross, cross_value).astype(jnp.bfloat16)
    biases = section_bias(azim_bias, azim_order, radials)

    def one_slice(index):
        start = index * BLOCK
        query_part = lax.dynamic_slice_in_dim(cross_queries, start, BLOCK, 1).reshape(line_count, BLOCK, HEADS, HEAD_DIM).astype(jnp.float32)
        key_part = lax.dynamic_slice_in_dim(cross_keys, start, BLOCK, 1).reshape(line_count, BLOCK, HEADS, HEAD_DIM).astype(jnp.float32)
        value_part = lax.dynamic_slice_in_dim(cross_values, start, BLOCK, 1).reshape(line_count, BLOCK, HEADS, HEAD_DIM).astype(jnp.float32)
        scores = jnp.einsum('aqhd,bqhd->qhab', query_part, key_part) + biases[None]
        weights = jnp.exp(scores)
        totals = lax.optimization_barrier(jnp.sum(weights, axis=-1))
        weighted = jnp.einsum('qhab,bqhd->aqhd', lowered(weights), value_part)
        result = weighted / jnp.transpose(totals, (2, 0, 1))[..., None]
        return result.reshape(line_count, BLOCK, width).astype(jnp.bfloat16)
    crossed = lax.map(one_slice, jnp.arange(stream_len // BLOCK, dtype=jnp.int32))
    crossed = jnp.transpose(crossed, (1, 0, 2, 3)).reshape(line_count, stream_len, width)
    result = (after_stream.astype(jnp.float32) + project(crossed, cross_out)).astype(jnp.bfloat16)
    return result.reshape(field.shape)
```

```python
import functools

import jax
import jax.numpy as jnp
from jax import lax
from jax.experimental import pallas as pl
from jax.experimental.pallas import tpu as pltpu
from jax.sharding import PartitionSpec as P

D = 256
HEADS = 4
HEAD_DIM = 64
BLOCK = 128
REACH = 2
LIST_LEN = 4
BLOCKS_DEV = 2
WINDOW = 2 * REACH + 1
LOG2E = 1.4426950408889634
CHUNKS = 2
OWN_MIB = 20
NEAR_MIB = 16
STREAM_MIB = 24
CROSS_MIB = 24
FINAL_MIB = 16
LANES = 128
SIDES = D // LANES
F32 = jnp.float32
BF16 = jnp.bfloat16


def shifted(block, distance):
    size = lax.axis_size("stream")
    return lax.ppermute(block, "stream", [((i - distance) % size, i) for i in range(size)])


def dot(left, right):
    return jnp.dot(left, right, preferred_element_type=F32)


def dot_t(left, right):
    return lax.dot_general(left, right, (((1,), (1,)), ((), ())), preferred_element_type=F32)


def normed_rows(values, gain_row):
    floats = values.astype(F32)
    mean = jnp.mean(floats * floats, axis=-1, keepdims=True)
    return (floats * lax.rsqrt(mean + 1e-05) * gain_row).astype(BF16)


def head_groups():
    rows = lax.broadcasted_iota(jnp.int32, (D, D), 0) // HEAD_DIM
    cols = lax.broadcasted_iota(jnp.int32, (D, D), 1) // HEAD_DIM
    return jnp.where(rows == cols, 1.0 / HEAD_DIM, 0.0).astype(BF16)


def head_factor(product, groups):
    square = product * product
    high = square.astype(BF16)
    low = (square - high.astype(F32)).astype(BF16)
    return lax.rsqrt(dot(high, groups) + dot(low, groups) + 1e-06)


def head_stack(queries):
    lane = lax.broadcasted_iota(jnp.int32, queries.shape, 1) // HEAD_DIM
    zero = jnp.zeros_like(queries)
    return jnp.concatenate([jnp.where(lane == h, queries, zero) for h in range(HEADS)], axis=0)


def attend(stack, keys, values, bias):
    scores = dot_t(stack, keys)
    if bias is not None:
        scores = scores + bias
    weights = jnp.exp2(scores)
    totals = jnp.sum(weights, axis=-1, keepdims=True)
    summed = dot(weights.astype(BF16), values) / totals
    count = stack.shape[0] // HEADS
    lane = lax.broadcasted_iota(jnp.int32, (count, D), 1) // HEAD_DIM
    result = summed[:count]
    for h in range(1, HEADS):
        result = jnp.where(lane == h, summed[h * count : (h + 1) * count], result)
    return result


def key_value(tokens, gain_row, key_weight, value_weight, groups):
    normed = normed_rows(tokens, gain_row)
    keys = dot(normed, key_weight)
    return (keys * head_factor(keys, groups)).astype(BF16), dot(normed, value_weight).astype(BF16)


def scale_row(scale_ref):
    head = lax.broadcasted_iota(jnp.int32, (1, D), 1) // HEAD_DIM
    row = jnp.zeros((1, D), F32)
    for h in range(HEADS):
        row = jnp.where(head == h, scale_ref[h] * (LOG2E / HEAD_DIM), row)
    return row


def fill_bias(order_ref, table_ref, bias_ref, per_azim):
    shape = (2 * HEAD_DIM, 2 * HEAD_DIM)
    azimuths = order_ref.shape[0]

    def placed(axis):
        row = per_azim(lax.broadcasted_iota(jnp.int32, shape, axis) % HEAD_DIM)
        found = jnp.zeros(shape, jnp.int32)
        for a in range(azimuths):
            found = jnp.where(row == a, order_ref[a], found)
        return found

    distance = placed(0) - placed(1)
    distance = jnp.where(distance < 0, distance + azimuths, distance)
    same = (lax.broadcasted_iota(jnp.int32, shape, 0) // HEAD_DIM) == (
        lax.broadcasted_iota(jnp.int32, shape, 1) // HEAD_DIM
    )
    distance = jnp.where(same, distance, -1)
    for h in range(HEADS):
        value = jnp.full(shape, -1e30, F32)
        for m in range(azimuths):
            value = jnp.where(distance == m, table_ref[h, m] * LOG2E, value)
        bias_ref[h * shape[0] : (h + 1) * shape[0]] = value


def own_kernel(
    scale_ref,
    order_ref,
    table_ref,
    field_ref,
    gain_ref,
    query_weight_ref,
    key_weight_ref,
    value_weight_ref,
    query_ref,
    kv_ref,
    bias_ref,
    *,
    per_azim,
):
    groups = head_groups()
    row = scale_row(scale_ref)
    fill_bias(order_ref, table_ref, bias_ref, per_azim)
    for line in range(field_ref.shape[0]):
        normed = normed_rows(field_ref[line], gain_ref[...])
        keys = dot(normed, key_weight_ref[...])
        kv_ref[line, :, :D] = (keys * head_factor(keys, groups)).astype(BF16)
        kv_ref[line, :, D:] = dot(normed, value_weight_ref[...]).astype(BF16)
        queries = dot(normed, query_weight_ref[...])
        query_ref[line] = (queries * head_factor(queries, groups) * row).astype(BF16)


def near_kernel(first_ref, second_ref, gain_ref, key_weight_ref, value_weight_ref, first_out, second_out):
    groups = head_groups()
    for source, target in ((first_ref, first_out), (second_ref, second_out)):
        for line in range(source.shape[0]):
            keys, values = key_value(
                source[line], gain_ref[...], key_weight_ref[...], value_weight_ref[...], groups
            )
            target[line, :, :D] = keys
            target[line, :, D:] = values


def stream_kernel(
    position_ref,
    list_ref,
    query_ref,
    field_ref,
    kv_own_ref,
    kv_next_ref,
    kv_prev_ref,
    far_next_ref,
    far_prev_ref,
    gain_ref,
    key_weight_ref,
    value_weight_ref,
    out_weight_ref,
    gain_cross_ref,
    *refs,
    first_line,
    size,
):
    after_ref, send_ref, window = refs[-3:]
    groups = head_groups()
    length = BLOCKS_DEV * BLOCK
    starts = []
    for block in range(BLOCKS_DEV):
        for j in range(LIST_LEN):
            named = list_ref[block, j]
            section = lax.rem(named // BLOCKS_DEV + REACH + size - position_ref[0], size)
            starts.append(section * length + (named % BLOCKS_DEV) * BLOCK)
    for line in range(far_next_ref.shape[0]):
        for place, source, at in (
            (1, kv_prev_ref, line),
            (2, kv_own_ref, first_line + line),
            (3, kv_next_ref, line),
        ):
            window[place * length : (place + 1) * length] = source[at]
        for place, source in ((0, far_prev_ref), (4, far_next_ref)):
            keys, values = key_value(
                source[line], gain_ref[...], key_weight_ref[...], value_weight_ref[...], groups
            )
            window[place * length : (place + 1) * length, :D] = keys
            window[place * length : (place + 1) * length, D:] = values
        parts = []
        for block in range(BLOCKS_DEV):
            stack = head_stack(query_ref[first_line + line, block * BLOCK : (block + 1) * BLOCK])
            picked = [
                window[pl.ds(pl.multiple_of(starts[block * LIST_LEN + j], BLOCK), BLOCK)]
                for j in range(LIST_LEN)
            ]
            listed = jnp.concatenate(picked, axis=0)
            parts.append(attend(stack, listed[:, :D], listed[:, D:], None))
        attended = jnp.concatenate(parts, axis=0).astype(BF16)
        fields = field_ref[first_line + line].astype(F32)
        after = (fields + dot(attended, out_weight_ref[...])).astype(BF16)
        after_ref[line] = after
        normed = normed_rows(after, gain_cross_ref[...])
        send_ref[:, first_line + line] = normed.reshape(send_ref.shape[:1] + send_ref.shape[2:])


def cross_kernel(
    scale_ref,
    source_ref,
    query_weight_ref,
    key_weight_ref,
    value_weight_ref,
    bias_ref,
    out_ref,
    gathered,
    result,
):
    groups = head_groups()
    row = scale_row(scale_ref)
    group, line_count, rows = out_ref.shape[:3]
    tokens = group * line_count
    block = source_ref[...].reshape(tokens * rows, D).astype(F32)
    for side in range(SIDES):
        gathered[side] = block[:, side * LANES : (side + 1) * LANES]
    for pair in range(rows // 2):
        both = jnp.concatenate(
            [
                jnp.concatenate(
                    [gathered[side, pl.ds(2 * pair + i, tokens, stride=rows)] for i in range(2)],
                    axis=0,
                )
                for side in range(SIDES)
            ],
            axis=1,
        ).astype(BF16)
        queries = dot(both, query_weight_ref[...])
        keys = dot(both, key_weight_ref[...])
        values = dot(both, value_weight_ref[...]).astype(BF16)
        queries = (queries * head_factor(queries, groups) * row).astype(BF16)
        keys = (keys * head_factor(keys, groups)).astype(BF16)
        attended = attend(head_stack(queries), keys, values, bias_ref[...])
        for i in range(2):
            for side in range(SIDES):
                result[side, pl.ds(2 * pair + i, tokens, stride=rows)] = attended[
                    i * tokens : (i + 1) * tokens, side * LANES : (side + 1) * LANES
                ]
    joined = jnp.concatenate([result[side] for side in range(SIDES)], axis=1)
    out_ref[...] = joined.astype(BF16).reshape(out_ref.shape)


def final_kernel(returned_ref, *refs):
    afters = refs[:CHUNKS]
    weight_ref, out_ref = refs[CHUNKS:]
    lines = out_ref.shape[0] // CHUNKS
    for line in range(out_ref.shape[0]):
        attended = returned_ref[:, line].reshape(-1, D)
        after = afters[line // lines][line % lines].astype(F32)
        out_ref[line] = (after + dot(attended, weight_ref[...])).astype(BF16)


VMEM = pl.BlockSpec(memory_space=pltpu.VMEM)
SMEM = pl.BlockSpec(memory_space=pltpu.SMEM)


def params(mib):
    return pltpu.CompilerParams(vmem_limit_bytes=mib << 20)


def cost(flops, nbytes, exps=0):
    return pl.CostEstimate(flops=flops, bytes_accessed=nbytes, transcendentals=exps)


def per_device(
    field,
    gain_stream,
    gain_cross,
    stream_query,
    stream_key,
    stream_value,
    stream_out,
    cross_query,
    cross_key,
    cross_value,
    cross_out,
    stream_scale,
    cross_scale,
    azim_bias,
    azim_order,
    block_lists,
):
    line_count = field.shape[0] * field.shape[1]
    length = field.shape[2]
    azims = lax.axis_size("azim")
    slabs = lax.axis_size("slab")
    group = azims * slabs
    rows = length // group
    lines = line_count // CHUNKS
    tokens = field.reshape(line_count, length, D)
    size = lax.axis_size("stream")

    pieces = [tokens[:lines]]
    for c in range(1, CHUNKS):
        held, _ = lax.optimization_barrier((tokens, pieces[-1]))
        pieces.append(held[c * lines : (c + 1) * lines])
    near = [(shifted(piece, 1), shifted(piece, -1)) for piece in pieces]
    far = [(shifted(ahead, 1), shifted(behind, -1)) for ahead, behind in near]

    gain_row = gain_stream.reshape(1, D)
    gain_cross_row = gain_cross.reshape(1, D)
    lines_per = field.shape[1]
    position = lax.axis_index("stream").astype(jnp.int32).reshape(1)

    def per_azim(token):
        device = token // line_count
        return (device // slabs) * field.shape[0] + (token % line_count) // lines_per

    shape = jax.ShapeDtypeStruct
    queries, kv_own, bias = pl.pallas_call(
        functools.partial(own_kernel, per_azim=per_azim),
        in_specs=[SMEM] * 3 + [VMEM] * 5,
        out_specs=[VMEM] * 3,
        out_shape=[
            shape((line_count, length, D), BF16),
            shape((line_count, length, 2 * D), BF16),
            shape((HEADS * 2 * HEAD_DIM, 2 * HEAD_DIM), F32),
        ],
        compiler_params=params(OWN_MIB),
        cost_estimate=cost(1 << 29, 1 << 21),
        name="own",
    )(stream_scale, azim_order, azim_bias, tokens, gain_row, stream_query, stream_key, stream_value)

    afters = []
    send = []
    for c in range(CHUNKS):
        kv_next, kv_prev = pl.pallas_call(
            near_kernel,
            in_specs=[VMEM] * 5,
            out_specs=[VMEM] * 2,
            out_shape=[shape((lines, length, 2 * D), BF16)] * 2,
            compiler_params=params(NEAR_MIB),
            cost_estimate=cost(1 << 28, 1 << 21),
            name="near",
        )(near[c][1], near[c][0], gain_row, stream_key, stream_value)
        after, *send = pl.pallas_call(
            functools.partial(stream_kernel, first_line=c * lines, size=size),
            in_specs=[SMEM] * 2 + [VMEM] * (12 + len(send)),
            out_specs=[VMEM] * 2,
            out_shape=[shape((lines, length, D), BF16), shape((group, line_count, rows, D), BF16)],
            input_output_aliases={14: 1} if send else {},
            scratch_shapes=[pltpu.VMEM((WINDOW * length, 2 * D), BF16)],
            compiler_params=params(STREAM_MIB),
            cost_estimate=cost(3 << 29, 1 << 22, 1 << 20),
            name="stream",
        )(
            position,
            block_lists,
            queries,
            tokens,
            kv_own,
            kv_next,
            kv_prev,
            far[c][1],
            far[c][0],
            gain_row,
            stream_key,
            stream_value,
            stream_out,
            gain_cross_row,
            *send,
        )
        afters.append(after)

    arrived = lax.all_to_all(send[0], ("azim", "slab"), 0, 0, tiled=True)
    crossed = pl.pallas_call(
        cross_kernel,
        in_specs=[SMEM] + [VMEM] * 5,
        out_specs=VMEM,
        out_shape=shape((group, line_count, rows, D), BF16),
        scratch_shapes=[pltpu.VMEM((SIDES, group * line_count * rows, LANES), F32)] * 2,
        compiler_params=params(CROSS_MIB),
        cost_estimate=cost(1 << 30, 1 << 21, 1 << 19),
        name="cross",
    )(cross_scale, arrived, cross_query, cross_key, cross_value, bias)
    returned = lax.all_to_all(crossed, ("azim", "slab"), 0, 0, tiled=True)

    result = pl.pallas_call(
        final_kernel,
        in_specs=[VMEM] * (2 + CHUNKS),
        out_specs=VMEM,
        out_shape=shape((line_count, length, D), BF16),
        compiler_params=params(FINAL_MIB),
        cost_estimate=cost(1 << 27, 3 << 19),
        name="final",
    )(returned, *afters, cross_out)
    return result.reshape(field.shape)


def solution(mesh):
    in_specs = (
        P("azim", "slab", "stream", None),
        P(),
        P(),
        P(),
        P(),
        P(),
        P(),
        P(),
        P(),
        P(),
        P(),
        P(),
        P(),
        P(),
        P(),
        P("stream", None),
    )
    out_specs = P("azim", "slab", "stream", None)
    return jax.shard_map(
        per_device, mesh=mesh, in_specs=in_specs, out_specs=out_specs, check_vma=False
    )
```

```python
import functools

import jax
import jax.numpy as jnp
from jax import lax
from jax.experimental import pallas as pl
from jax.experimental.pallas import tpu as pltpu
from jax.sharding import PartitionSpec as P

D = 256
HEADS = 4
HEAD_DIM = 64
BLOCK = 128
REACH = 2
LIST_LEN = 4
BLOCKS_DEV = 2
WINDOW = 2 * REACH + 1
LOG2E = 1.4426950408889634
CHUNKS = 2
FETCHED = 7
OWN_MIB = 20
NEAR_MIB = 16
STREAM_MIB = 24
CROSS_MIB = 24
FINAL_MIB = 16
LANES = 128
SIDES = D // LANES
F32 = jnp.float32
BF16 = jnp.bfloat16


def shifted(block, distance):
    size = lax.axis_size("stream")
    return lax.ppermute(block, "stream", [((i - distance) % size, i) for i in range(size)])


def dot(left, right):
    return jnp.dot(left, right, preferred_element_type=F32)


def dot_t(left, right):
    return lax.dot_general(left, right, (((1,), (1,)), ((), ())), preferred_element_type=F32)


def normed_rows(values, gain_row):
    floats = values.astype(F32)
    mean = jnp.mean(floats * floats, axis=-1, keepdims=True)
    return (floats * lax.rsqrt(mean + 1e-05) * gain_row).astype(BF16)


def head_groups():
    rows = lax.broadcasted_iota(jnp.int32, (D, D), 0) // HEAD_DIM
    cols = lax.broadcasted_iota(jnp.int32, (D, D), 1) // HEAD_DIM
    return jnp.where(rows == cols, 1.0 / HEAD_DIM, 0.0).astype(BF16)


def head_units(product, groups):
    means = dot((product * product).astype(BF16), groups)
    return product * lax.rsqrt(means + 1e-06)


def head_stack(queries):
    lane = lax.broadcasted_iota(jnp.int32, queries.shape, 1) // HEAD_DIM
    zero = jnp.zeros_like(queries)
    return jnp.concatenate([jnp.where(lane == h, queries, zero) for h in range(HEADS)], axis=0)


def attend(stack, keys, values, bias):
    scores = dot_t(stack, keys)
    if bias is not None:
        scores = scores + bias
    weights = jnp.exp2(scores)
    factors = 1.0 / jnp.sum(weights, axis=-1, keepdims=True)
    summed = dot(weights.astype(BF16), values)
    count = stack.shape[0] // HEADS
    lane = lax.broadcasted_iota(jnp.int32, (count, D), 1) // HEAD_DIM
    result = summed[:count]
    factor = jnp.broadcast_to(factors[:count], (count, D))
    for h in range(1, HEADS):
        at = slice(h * count, (h + 1) * count)
        result = jnp.where(lane == h, summed[at], result)
        factor = jnp.where(lane == h, factors[at], factor)
    return result * factor


def scale_row(scale_ref):
    head = lax.broadcasted_iota(jnp.int32, (1, D), 1) // HEAD_DIM
    row = jnp.zeros((1, D), F32)
    for h in range(HEADS):
        row = jnp.where(head == h, scale_ref[h] * (LOG2E / HEAD_DIM), row)
    return row


def prepare_kernel(position_ref, *refs, per_azim, size):
    small, fetched, refs = refs[:5], refs[5 : 5 + FETCHED], refs[5 + FETCHED :]
    stream_row_ref, cross_row_ref, start_ref, bias_ref = refs[:4]
    held, refs = refs[4 : 4 + FETCHED], refs[4 + FETCHED :]
    stream_scale_ref, cross_scale_ref, order_ref, table_ref, list_ref, sems = refs
    copies = [
        pltpu.make_async_copy(source, target, sems.at[i])
        for i, (source, target) in enumerate(zip(small + fetched, refs[:5] + held))
    ]
    for copy in copies:
        copy.start()
    for copy in copies[:5]:
        copy.wait()
    stream_row_ref[...] = scale_row(stream_scale_ref)
    cross_row_ref[...] = scale_row(cross_scale_ref)
    for block in range(BLOCKS_DEV):
        for j in range(LIST_LEN):
            named = list_ref[block, j]
            section = lax.rem(named // BLOCKS_DEV + (REACH + size) - position_ref[0], size)
            start_ref[block, j] = section * (BLOCKS_DEV * BLOCK) + (named % BLOCKS_DEV) * BLOCK
    shape = (2 * HEAD_DIM, 2 * HEAD_DIM)
    azimuths = order_ref.shape[0]

    def placed(axis):
        dims = (shape[0], 1) if axis == 0 else (1, shape[1])
        row = per_azim(lax.broadcasted_iota(jnp.int32, dims, axis) % HEAD_DIM)
        found = jnp.zeros(dims, jnp.int32)
        for a in range(azimuths):
            found = jnp.where(row == a, order_ref[a], found)
        return found

    distance = placed(0) - placed(1)
    distance = jnp.where(distance < 0, distance + azimuths, distance)
    same = (lax.broadcasted_iota(jnp.int32, shape, 0) // HEAD_DIM) == (
        lax.broadcasted_iota(jnp.int32, shape, 1) // HEAD_DIM
    )
    distance = jnp.where(same, distance, -1)
    for h in range(HEADS):
        value = jnp.full(shape, -1e30, F32)
        for m in range(azimuths):
            value = jnp.where(distance == m, table_ref[h, m] * LOG2E, value)
        bias_ref[h * shape[0] : (h + 1) * shape[0]] = value
    for copy in copies[5:]:
        copy.wait()


def own_kernel(row_ref, field_ref, gain_ref, query_weight_ref, key_weight_ref, value_weight_ref, query_ref, kv_ref):
    lines, length = field_ref.shape[:2]
    groups = head_groups()
    normed = normed_rows(field_ref[...].reshape(-1, D), gain_ref[...])
    keys = head_units(dot(normed, key_weight_ref[...]), groups).astype(BF16)
    kv_ref[:, :, :D] = keys.reshape(lines, length, D)
    queries = head_units(dot(normed, query_weight_ref[...]), groups) * row_ref[...]
    query_ref[...] = queries.astype(BF16).reshape(lines, length, D)
    kv_ref[:, :, D:] = dot(normed, value_weight_ref[...]).astype(BF16).reshape(lines, length, D)


def near_kernel(prev_ref, next_ref, own_ref, gain_ref, key_weight_ref, value_weight_ref, out_ref, *, first_line):
    lines, length = prev_ref.shape[:2]
    groups = head_groups()
    tokens = jnp.concatenate([prev_ref[...].reshape(-1, D), next_ref[...].reshape(-1, D)], axis=0)
    normed = normed_rows(tokens, gain_ref[...])
    keys = head_units(dot(normed, key_weight_ref[...]), groups).astype(BF16)
    values = dot(normed, value_weight_ref[...]).astype(BF16)
    half = lines * length
    for part, place in ((0, 0), (1, 2)):
        at = slice(place * length, (place + 1) * length)
        out_ref[:, at, :D] = keys[part * half : (part + 1) * half].reshape(lines, length, D)
        out_ref[:, at, D:] = values[part * half : (part + 1) * half].reshape(lines, length, D)
    out_ref[:, length : 2 * length] = own_ref[first_line : first_line + lines]


def stream_kernel(
    start_ref,
    query_ref,
    field_ref,
    window_ref,
    far_prev_ref,
    far_next_ref,
    gain_ref,
    key_weight_ref,
    value_weight_ref,
    out_weight_ref,
    gain_cross_ref,
    *refs,
    first_line,
):
    after_ref, send_ref, far = refs[-3:]
    earlier = refs[:-3]
    lines, length = far_prev_ref.shape[:2]
    groups = head_groups()
    tokens = jnp.concatenate(
        [far_prev_ref[...].reshape(-1, D), far_next_ref[...].reshape(-1, D)], axis=0
    )
    normed = normed_rows(tokens, gain_ref[...])
    far[:, :D] = head_units(dot(normed, key_weight_ref[...]), groups).astype(BF16)
    far[:, D:] = dot(normed, value_weight_ref[...]).astype(BF16)
    near_rows = window_ref.shape[1]
    parts = []
    for line in range(lines):
        for block in range(BLOCKS_DEV):
            stack = head_stack(query_ref[first_line + line, block * BLOCK : (block + 1) * BLOCK])
            picked = []
            for j in range(LIST_LEN):
                start = start_ref[block, j]
                before = start < length
                after = start >= length + near_rows
                near_at = jnp.where(before | after, 0, start - length)
                far_at = line * length + jnp.where(
                    before, start, jnp.where(after, start - (length + near_rows) + lines * length, 0)
                )
                close = window_ref[line, pl.ds(pl.multiple_of(near_at, BLOCK), BLOCK)]
                distant = far[pl.ds(pl.multiple_of(far_at, BLOCK), BLOCK)]
                picked.append(jnp.where(before | after, distant, close))
            listed = jnp.concatenate(picked, axis=0)
            parts.append(attend(stack, listed[:, :D], listed[:, D:], None))
    attended = jnp.concatenate(parts, axis=0).astype(BF16)
    fields = field_ref[first_line : first_line + lines].reshape(-1, D).astype(F32)
    after = (fields + dot(attended, out_weight_ref[...])).astype(BF16)
    after_ref[...] = after.reshape(lines, length, D)
    normed = normed_rows(after, gain_cross_ref[...])
    group, _, rows, _ = send_ref.shape
    for line in range(lines):
        send_ref[:, first_line + line] = normed[line * length : (line + 1) * length].reshape(
            group, rows, D
        )
    for previous in earlier:
        send_ref[:, :first_line] = previous[:, :first_line]


def cross_kernel(
    row_ref,
    source_ref,
    query_weight_ref,
    key_weight_ref,
    value_weight_ref,
    bias_ref,
    out_ref,
    mixed,
    ordered,
    query_buffer,
    key_buffer,
    value_buffer,
):
    groups = head_groups()
    group, line_count, rows = out_ref.shape[:3]
    tokens = group * line_count
    block = source_ref[...].reshape(tokens * rows, D).astype(F32)
    for side in range(SIDES):
        mixed[side] = block[:, side * LANES : (side + 1) * LANES]
    for index in range(rows):
        at = slice(index * tokens, (index + 1) * tokens)
        ordered[at] = jnp.concatenate(
            [mixed[side, pl.ds(index, tokens, stride=rows)] for side in range(SIDES)], axis=1
        ).astype(BF16)
    normed = ordered[...]
    key_buffer[...] = head_units(dot(normed, key_weight_ref[...]), groups).astype(BF16)
    query_buffer[...] = (
        head_units(dot(normed, query_weight_ref[...]), groups) * row_ref[...]
    ).astype(BF16)
    value_buffer[...] = dot(normed, value_weight_ref[...]).astype(BF16)
    for pair in range(rows // 2):
        at = slice(2 * pair * tokens, (2 * pair + 2) * tokens)
        attended = attend(
            head_stack(query_buffer[at]), key_buffer[at], value_buffer[at], bias_ref[...]
        )
        for i in range(2):
            for side in range(SIDES):
                mixed[side, pl.ds(2 * pair + i, tokens, stride=rows)] = attended[
                    i * tokens : (i + 1) * tokens, side * LANES : (side + 1) * LANES
                ]
    joined = jnp.concatenate([mixed[side] for side in range(SIDES)], axis=1)
    out_ref[...] = joined.astype(BF16).reshape(out_ref.shape)


def final_kernel(returned_ref, *refs):
    afters = refs[:CHUNKS]
    weight_ref, out_ref = refs[CHUNKS:]
    line_count, length = out_ref.shape[:2]
    lines = line_count // CHUNKS
    attended = jnp.concatenate(
        [returned_ref[:, line].reshape(-1, D) for line in range(line_count)], axis=0
    )
    after = jnp.concatenate([part[...].reshape(-1, D) for part in afters], axis=0).astype(F32)
    out_ref[...] = (after + dot(attended, weight_ref[...])).astype(BF16).reshape(out_ref.shape)


VMEM = pl.BlockSpec(memory_space=pltpu.VMEM)
SMEM = pl.BlockSpec(memory_space=pltpu.SMEM)


def params(mib):
    return pltpu.CompilerParams(vmem_limit_bytes=mib << 20)


def cost(flops, nbytes, exps=0):
    return pl.CostEstimate(flops=flops, bytes_accessed=nbytes, transcendentals=exps)


def per_device(
    field,
    gain_stream,
    gain_cross,
    stream_query,
    stream_key,
    stream_value,
    stream_out,
    cross_query,
    cross_key,
    cross_value,
    cross_out,
    stream_scale,
    cross_scale,
    azim_bias,
    azim_order,
    block_lists,
):
    line_count = field.shape[0] * field.shape[1]
    length = field.shape[2]
    azims = lax.axis_size("azim")
    slabs = lax.axis_size("slab")
    group = azims * slabs
    rows = length // group
    lines = line_count // CHUNKS
    tokens = field.reshape(line_count, length, D)
    size = lax.axis_size("stream")

    pieces = [tokens[:lines]]
    for c in range(1, CHUNKS):
        held, _ = lax.optimization_barrier((tokens, pieces[-1]))
        pieces.append(held[c * lines : (c + 1) * lines])
    near = [(shifted(piece, 1), shifted(piece, -1)) for piece in pieces]

    gain_row = gain_stream.reshape(1, D)
    gain_cross_row = gain_cross.reshape(1, D)
    lines_per = field.shape[1]
    position = lax.axis_index("stream").astype(jnp.int32).reshape(1)

    def per_azim(token):
        device = token // line_count
        return (device // slabs) * field.shape[0] + (token % line_count) // lines_per

    shape = jax.ShapeDtypeStruct
    small = [stream_scale, cross_scale, azim_order, azim_bias, block_lists]
    fetched = [tokens, gain_row, gain_cross_row, stream_query, stream_key, stream_value, stream_out]
    stream_row, cross_row, starts, bias, *held = pl.pallas_call(
        functools.partial(prepare_kernel, per_azim=per_azim, size=size),
        in_specs=[SMEM] + [pl.BlockSpec(memory_space=pltpu.HBM)] * (5 + FETCHED),
        out_specs=[VMEM, VMEM, SMEM, VMEM] + [VMEM] * FETCHED,
        out_shape=[
            shape((1, D), F32),
            shape((1, D), F32),
            shape(block_lists.shape, jnp.int32),
            shape((HEADS * 2 * HEAD_DIM, 2 * HEAD_DIM), F32),
        ]
        + [shape(array.shape, array.dtype) for array in fetched],
        scratch_shapes=[pltpu.SMEM(array.shape, array.dtype) for array in small]
        + [pltpu.SemaphoreType.DMA((5 + FETCHED,))],
        compiler_params=params(NEAR_MIB),
        cost_estimate=cost(1 << 20, 1 << 18),
        name="prepare",
    )(position, *[pltpu.with_memory_space_constraint(array, pltpu.HBM) for array in small + fetched])
    tokens, gain_row, gain_cross_row, stream_query, stream_key, stream_value, stream_out = held

    far = []
    for c, (ahead, behind) in enumerate(near):
        if c == 0:
            ahead, behind, _ = lax.optimization_barrier((ahead, behind, cross_row))
        far.append((shifted(ahead, 1), shifted(behind, -1)))

    queries, kv_own = pl.pallas_call(
        own_kernel,
        in_specs=[VMEM] * 6,
        out_specs=[VMEM] * 2,
        out_shape=[
            shape((line_count, length, D), BF16),
            shape((line_count, length, 2 * D), BF16),
        ],
        compiler_params=params(OWN_MIB),
        cost_estimate=cost(1 << 29, 1 << 21),
        name="own",
    )(stream_row, tokens, gain_row, stream_query, stream_key, stream_value)

    afters = []
    send = []
    for c in range(CHUNKS):
        window = pl.pallas_call(
            functools.partial(near_kernel, first_line=c * lines),
            in_specs=[VMEM] * 6,
            out_specs=VMEM,
            out_shape=shape((lines, 3 * length, 2 * D), BF16),
            compiler_params=params(NEAR_MIB),
            cost_estimate=cost(1 << 28, 1 << 21),
            name="near",
        )(near[c][0], near[c][1], kv_own, gain_row, stream_key, stream_value)
        after, *send = pl.pallas_call(
            functools.partial(stream_kernel, first_line=c * lines),
            in_specs=[SMEM] + [VMEM] * (10 + len(send)),
            out_specs=[VMEM] * 2,
            out_shape=[shape((lines, length, D), BF16), shape((group, line_count, rows, D), BF16)],
            scratch_shapes=[pltpu.VMEM((2 * lines * length, 2 * D), BF16)],
            compiler_params=params(STREAM_MIB),
            cost_estimate=cost(3 << 29, 1 << 22, 1 << 20),
            name="stream",
        )(
            starts,
            queries,
            tokens,
            window,
            far[c][0],
            far[c][1],
            gain_row,
            stream_key,
            stream_value,
            stream_out,
            gain_cross_row,
            *send,
        )
        afters.append(after)

    arrived = lax.all_to_all(send[0], ("azim", "slab"), 0, 0, tiled=True)
    crossed = pl.pallas_call(
        cross_kernel,
        in_specs=[VMEM] * 6,
        out_specs=VMEM,
        out_shape=shape((group, line_count, rows, D), BF16),
        scratch_shapes=[pltpu.VMEM((SIDES, group * line_count * rows, LANES), F32)]
        + [pltpu.VMEM((group * line_count * rows, D), BF16)] * 4,
        compiler_params=params(CROSS_MIB),
        cost_estimate=cost(1 << 30, 1 << 21, 1 << 19),
        name="cross",
    )(cross_row, arrived, cross_query, cross_key, cross_value, bias)
    returned = lax.all_to_all(crossed, ("azim", "slab"), 0, 0, tiled=True)

    result = pl.pallas_call(
        final_kernel,
        in_specs=[VMEM] * (2 + CHUNKS),
        out_specs=VMEM,
        out_shape=shape((line_count, length, D), BF16),
        compiler_params=params(FINAL_MIB),
        cost_estimate=cost(1 << 27, 3 << 19),
        name="final",
    )(returned, *afters, cross_out)
    return result.reshape(field.shape)


def solution(mesh):
    in_specs = (
        P("azim", "slab", "stream", None),
        P(),
        P(),
        P(),
        P(),
        P(),
        P(),
        P(),
        P(),
        P(),
        P(),
        P(),
        P(),
        P(),
        P(),
        P("stream", None),
    )
    out_specs = P("azim", "slab", "stream", None)
    return jax.shard_map(
        per_device, mesh=mesh, in_specs=in_specs, out_specs=out_specs, check_vma=False
    )
```

```python
import functools

import jax
import jax.numpy as jnp
from jax import lax
from jax.experimental import pallas as pl
from jax.experimental.pallas import tpu as pltpu
from jax.sharding import PartitionSpec as P

D = 256
HEADS = 4
HEAD_DIM = 64
BLOCK = 128
REACH = 2
LIST_LEN = 4
BLOCKS_DEV = 2
WINDOW = 2 * REACH + 1
LOG2E = 1.4426950408889634
CHUNKS = 2
FETCHED = 7
OWN_MIB = 20
NEAR_MIB = 16
STREAM_MIB = 24
CROSS_MIB = 24
FINAL_MIB = 16
F32 = jnp.float32
BF16 = jnp.bfloat16


def shifted(block, distance):
    size = lax.axis_size("stream")
    return lax.ppermute(block, "stream", [((i - distance) % size, i) for i in range(size)])


def dot(left, right):
    return jnp.dot(left, right, preferred_element_type=F32)


def dot_t(left, right):
    return lax.dot_general(left, right, (((1,), (1,)), ((), ())), preferred_element_type=F32)


def normed_rows(values, gain_row):
    floats = values.astype(F32)
    mean = jnp.mean(floats * floats, axis=-1, keepdims=True)
    return (floats * lax.rsqrt(mean + 1e-05) * gain_row).astype(BF16)


def head_groups():
    rows = lax.broadcasted_iota(jnp.int32, (D, D), 0) // HEAD_DIM
    cols = lax.broadcasted_iota(jnp.int32, (D, D), 1) // HEAD_DIM
    return jnp.where(rows == cols, 1.0 / HEAD_DIM, 0.0).astype(BF16)


def head_units(product, groups):
    means = dot((product * product).astype(BF16), groups)
    return product * lax.rsqrt(means + 1e-06)


def head_stack(queries):
    lane = lax.broadcasted_iota(jnp.int32, queries.shape, 1) // HEAD_DIM
    zero = jnp.zeros_like(queries)
    return jnp.concatenate([jnp.where(lane == h, queries, zero) for h in range(HEADS)], axis=0)


def attend(stack, keys, values):
    weights = jnp.exp2(dot_t(stack, keys))
    factors = 1.0 / jnp.sum(weights, axis=-1, keepdims=True)
    summed = dot(weights.astype(BF16), values)
    count = stack.shape[0] // HEADS
    lane = lax.broadcasted_iota(jnp.int32, (count, D), 1) // HEAD_DIM
    result = summed[:count]
    factor = jnp.broadcast_to(factors[:count], (count, D))
    for h in range(1, HEADS):
        at = slice(h * count, (h + 1) * count)
        result = jnp.where(lane == h, summed[at], result)
        factor = jnp.where(lane == h, factors[at], factor)
    return result * factor


def scale_row(scale_ref):
    head = lax.broadcasted_iota(jnp.int32, (1, D), 1) // HEAD_DIM
    row = jnp.zeros((1, D), F32)
    for h in range(HEADS):
        row = jnp.where(head == h, scale_ref[h] * (LOG2E / HEAD_DIM), row)
    return row


def prepare_kernel(position_ref, *refs, per_azim, size):
    small, fetched, refs = refs[:5], refs[5 : 5 + FETCHED], refs[5 + FETCHED :]
    stream_row_ref, cross_row_ref, start_ref, bias_ref = refs[:4]
    held, refs = refs[4 : 4 + FETCHED], refs[4 + FETCHED :]
    stream_scale_ref, cross_scale_ref, order_ref, table_ref, list_ref, sems = refs
    copies = [
        pltpu.make_async_copy(source, target, sems.at[i])
        for i, (source, target) in enumerate(zip(small + fetched, refs[:5] + held))
    ]
    for copy in copies:
        copy.start()
    for copy in copies[:5]:
        copy.wait()
    stream_row_ref[...] = scale_row(stream_scale_ref)
    cross_row_ref[...] = scale_row(cross_scale_ref)
    for block in range(BLOCKS_DEV):
        for j in range(LIST_LEN):
            named = list_ref[block, j]
            section = lax.rem(named // BLOCKS_DEV + (REACH + size) - position_ref[0], size)
            start_ref[block, j] = section * (BLOCKS_DEV * BLOCK) + (named % BLOCKS_DEV) * BLOCK
    tokens = bias_ref.shape[0]
    azimuths = order_ref.shape[0]

    def placed(axis):
        dims = (tokens, 1) if axis == 0 else (1, HEADS * tokens)
        row = per_azim(lax.broadcasted_iota(jnp.int32, dims, axis) % tokens)
        found = jnp.zeros(dims, jnp.int32)
        for a in range(azimuths):
            found = jnp.where(row == a, order_ref[a], found)
        return found

    distance = placed(0) - placed(1)
    distance = jnp.where(distance < 0, distance + azimuths, distance)
    head = lax.broadcasted_iota(jnp.int32, (1, HEADS * tokens), 1) // tokens
    value = jnp.zeros(bias_ref.shape, F32)
    for m in range(azimuths):
        row = jnp.zeros((1, HEADS * tokens), F32)
        for h in range(HEADS):
            row = jnp.where(head == h, table_ref[h, m] * LOG2E, row)
        value = jnp.where(distance == m, row, value)
    bias_ref[...] = value
    for copy in copies[5:]:
        copy.wait()


def own_kernel(row_ref, field_ref, gain_ref, query_weight_ref, key_weight_ref, value_weight_ref, query_ref, kv_ref):
    lines, length = field_ref.shape[:2]
    groups = head_groups()
    normed = normed_rows(field_ref[...].reshape(-1, D), gain_ref[...])
    keys = head_units(dot(normed, key_weight_ref[...]), groups).astype(BF16)
    kv_ref[:, :, :D] = keys.reshape(lines, length, D)
    queries = head_units(dot(normed, query_weight_ref[...]), groups) * row_ref[...]
    query_ref[...] = queries.astype(BF16).reshape(lines, length, D)
    kv_ref[:, :, D:] = dot(normed, value_weight_ref[...]).astype(BF16).reshape(lines, length, D)


def near_kernel(prev_ref, next_ref, own_ref, gain_ref, key_weight_ref, value_weight_ref, out_ref, *, first_line):
    lines, length = prev_ref.shape[:2]
    groups = head_groups()
    tokens = jnp.concatenate([prev_ref[...].reshape(-1, D), next_ref[...].reshape(-1, D)], axis=0)
    normed = normed_rows(tokens, gain_ref[...])
    keys = head_units(dot(normed, key_weight_ref[...]), groups).astype(BF16)
    values = dot(normed, value_weight_ref[...]).astype(BF16)
    half = lines * length
    for part, place in ((0, 0), (1, 2)):
        at = slice(place * length, (place + 1) * length)
        out_ref[:, at, :D] = keys[part * half : (part + 1) * half].reshape(lines, length, D)
        out_ref[:, at, D:] = values[part * half : (part + 1) * half].reshape(lines, length, D)
    out_ref[:, length : 2 * length] = own_ref[first_line : first_line + lines]


def lines_of(ref):
    return ref.shape[0]


def stream_kernel(
    start_ref,
    query_ref,
    field_ref,
    window_ref,
    far_prev_ref,
    far_next_ref,
    gain_ref,
    key_weight_ref,
    value_weight_ref,
    out_weight_ref,
    gain_cross_ref,
    *refs,
    first_line,
):
    after_ref, send_ref, *far = refs[-2 - lines_of(far_prev_ref) :]
    earlier = refs[: -2 - lines_of(far_prev_ref)]
    lines, length = far_prev_ref.shape[:2]
    groups = head_groups()
    near_rows = window_ref.shape[1]
    group, _, rows, _ = send_ref.shape

    def project(line):
        tokens = jnp.concatenate([far_prev_ref[line], far_next_ref[line]], axis=0)
        normed = normed_rows(tokens, gain_ref[...])
        far[line][:, :D] = head_units(dot(normed, key_weight_ref[...]), groups).astype(BF16)
        far[line][:, D:] = dot(normed, value_weight_ref[...]).astype(BF16)

    def attended(line):
        parts = []
        for block in range(BLOCKS_DEV):
            stack = head_stack(query_ref[first_line + line, block * BLOCK : (block + 1) * BLOCK])
            picked = []
            for j in range(LIST_LEN):
                start = start_ref[block, j]
                before = start < length
                after = start >= length + near_rows
                near_at = jnp.where(before | after, 0, start - length)
                far_at = jnp.where(before, start, jnp.where(after, start - near_rows, 0))
                close = window_ref[line, pl.ds(pl.multiple_of(near_at, BLOCK), BLOCK)]
                distant = far[line][pl.ds(pl.multiple_of(far_at, BLOCK), BLOCK)]
                picked.append(jnp.where(before | after, distant, close))
            listed = jnp.concatenate(picked, axis=0)
            parts.append(attend(stack, listed[:, :D], listed[:, D:]))
        return jnp.concatenate(parts, axis=0).astype(BF16)

    def finish(some, rows_in):
        fields = field_ref[first_line + some.start : first_line + some.stop].reshape(-1, D).astype(F32)
        after = (fields + dot(rows_in, out_weight_ref[...])).astype(BF16)
        after_ref[some] = after.reshape(-1, length, D)
        normed = normed_rows(after, gain_cross_ref[...])
        for line in range(some.start, some.stop):
            at = (line - some.start) * length
            send_ref[:, first_line + line] = normed[at : at + length].reshape(group, rows, D)

    for line in range(lines):
        project(line)
    finish(slice(0, lines), jnp.concatenate([attended(line) for line in range(lines)], axis=0))
    for previous in earlier:
        send_ref[:, :first_line] = previous[:, :first_line]


def turned(block, turn, rows):
    return dot(turn, block.reshape(rows * rows, D)).astype(BF16)


def cross_kernel(
    row_ref,
    source_ref,
    query_weight_ref,
    key_weight_ref,
    value_weight_ref,
    bias_ref,
    out_ref,
    ordered,
):
    groups = head_groups()
    group, line_count, rows = out_ref.shape[:3]
    tokens = group * line_count
    square = rows * rows
    to_row = lax.broadcasted_iota(jnp.int32, (square, square), 0)
    from_row = lax.broadcasted_iota(jnp.int32, (square, square), 1)
    turn = jnp.where(from_row == (to_row % rows) * rows + to_row // rows, 1.0, 0.0).astype(BF16)
    source = source_ref[...].reshape(tokens * rows, D)
    joint = lax.broadcasted_iota(jnp.int32, (HEADS * tokens, D), 0) // tokens
    summing = jnp.where(
        joint == lax.broadcasted_iota(jnp.int32, (HEADS * tokens, D), 1) // HEAD_DIM, 1.0, 0.0
    ).astype(BF16)
    for at in range(0, tokens, rows):
        block = turned(source[at * rows : (at + rows) * rows], turn, rows)
        ordered[:, at : at + rows] = block.reshape(rows, rows, D)
    normed = ordered[...].reshape(rows * tokens, D)
    keys = head_units(dot(normed, key_weight_ref[...]), groups).astype(BF16)
    queries = (head_units(dot(normed, query_weight_ref[...]), groups) * row_ref[...]).astype(BF16)
    values = dot(normed, value_weight_ref[...]).astype(BF16)
    spans = [slice(index * tokens, (index + 1) * tokens) for index in range(rows)]
    weights = []
    for at in spans:
        scores = dot_t(queries[at], head_stack(keys[at])) + bias_ref[...]
        weights.append(jnp.exp2(scores).astype(BF16))
    totals = dot(jnp.concatenate(weights, axis=0), summing)
    summed = jnp.concatenate(
        [dot(part, head_stack(values[at])) for part, at in zip(weights, spans)], axis=0
    )
    ordered[...] = (summed / totals).astype(BF16).reshape(rows, tokens, D)
    lines = rows // line_count
    for at in range(0, tokens, rows):
        block = turned(ordered[:, at : at + rows], turn, rows)
        out_ref[at // line_count : at // line_count + lines] = block.reshape(
            lines, line_count, rows, D
        )


def final_kernel(returned_ref, *refs):
    afters = refs[:CHUNKS]
    weight_ref, out_ref = refs[CHUNKS:]
    line_count, length = out_ref.shape[:2]
    lines = line_count // CHUNKS
    attended = jnp.concatenate(
        [returned_ref[:, line].reshape(-1, D) for line in range(line_count)], axis=0
    )
    after = jnp.concatenate([part[...].reshape(-1, D) for part in afters], axis=0).astype(F32)
    out_ref[...] = (after + dot(attended, weight_ref[...])).astype(BF16).reshape(out_ref.shape)


VMEM = pl.BlockSpec(memory_space=pltpu.VMEM)
SMEM = pl.BlockSpec(memory_space=pltpu.SMEM)


def params(mib):
    return pltpu.CompilerParams(vmem_limit_bytes=mib << 20)


def cost(flops, nbytes, exps=0):
    return pl.CostEstimate(flops=flops, bytes_accessed=nbytes, transcendentals=exps)


def per_device(
    field,
    gain_stream,
    gain_cross,
    stream_query,
    stream_key,
    stream_value,
    stream_out,
    cross_query,
    cross_key,
    cross_value,
    cross_out,
    stream_scale,
    cross_scale,
    azim_bias,
    azim_order,
    block_lists,
):
    line_count = field.shape[0] * field.shape[1]
    length = field.shape[2]
    azims = lax.axis_size("azim")
    slabs = lax.axis_size("slab")
    group = azims * slabs
    rows = length // group
    lines = line_count // CHUNKS
    tokens = field.reshape(line_count, length, D)
    size = lax.axis_size("stream")

    pieces = [tokens[:lines]]
    for c in range(1, CHUNKS):
        held, _ = lax.optimization_barrier((tokens, pieces[-1]))
        pieces.append(held[c * lines : (c + 1) * lines])
    near = [(shifted(piece, 1), shifted(piece, -1)) for piece in pieces]

    gain_row = gain_stream.reshape(1, D)
    gain_cross_row = gain_cross.reshape(1, D)
    lines_per = field.shape[1]
    position = lax.axis_index("stream").astype(jnp.int32).reshape(1)

    def per_azim(token):
        device = token // line_count
        return (device % azims) * field.shape[0] + (token % line_count) // lines_per

    shape = jax.ShapeDtypeStruct
    small = [stream_scale, cross_scale, azim_order, azim_bias, block_lists]
    fetched = [tokens, gain_row, gain_cross_row, stream_query, stream_key, stream_value, stream_out]
    stream_row, cross_row, starts, bias, *held = pl.pallas_call(
        functools.partial(prepare_kernel, per_azim=per_azim, size=size),
        in_specs=[SMEM] + [pl.BlockSpec(memory_space=pltpu.HBM)] * (5 + FETCHED),
        out_specs=[VMEM, VMEM, SMEM, VMEM] + [VMEM] * FETCHED,
        out_shape=[
            shape((1, D), F32),
            shape((1, D), F32),
            shape(block_lists.shape, jnp.int32),
            shape((group * line_count, HEADS * group * line_count), F32),
        ]
        + [shape(array.shape, array.dtype) for array in fetched],
        scratch_shapes=[pltpu.SMEM(array.shape, array.dtype) for array in small]
        + [pltpu.SemaphoreType.DMA((5 + FETCHED,))],
        compiler_params=params(NEAR_MIB),
        cost_estimate=cost(1 << 20, 1 << 18),
        name="prepare",
    )(position, *[pltpu.with_memory_space_constraint(array, pltpu.HBM) for array in small + fetched])
    tokens, gain_row, gain_cross_row, stream_query, stream_key, stream_value, stream_out = held

    far = []
    for c, (ahead, behind) in enumerate(near):
        if c == 0:
            ahead, behind, _ = lax.optimization_barrier((ahead, behind, cross_row))
        far.append((shifted(ahead, 1), shifted(behind, -1)))

    queries, kv_own = pl.pallas_call(
        own_kernel,
        in_specs=[VMEM] * 6,
        out_specs=[VMEM] * 2,
        out_shape=[
            shape((line_count, length, D), BF16),
            shape((line_count, length, 2 * D), BF16),
        ],
        compiler_params=params(OWN_MIB),
        cost_estimate=cost(1 << 29, 1 << 21),
        name="own",
    )(stream_row, tokens, gain_row, stream_query, stream_key, stream_value)

    afters = []
    send = []
    for c in range(CHUNKS):
        window = pl.pallas_call(
            functools.partial(near_kernel, first_line=c * lines),
            in_specs=[VMEM] * 6,
            out_specs=VMEM,
            out_shape=shape((lines, 3 * length, 2 * D), BF16),
            compiler_params=params(NEAR_MIB),
            cost_estimate=cost(1 << 28, 1 << 21),
            name="near",
        )(near[c][0], near[c][1], kv_own, gain_row, stream_key, stream_value)
        after, *send = pl.pallas_call(
            functools.partial(stream_kernel, first_line=c * lines),
            in_specs=[SMEM] + [VMEM] * (10 + len(send)),
            out_specs=[VMEM] * 2,
            out_shape=[shape((lines, length, D), BF16), shape((group, line_count, rows, D), BF16)],
            scratch_shapes=[pltpu.VMEM((2 * length, 2 * D), BF16)] * lines,
            compiler_params=params(STREAM_MIB),
            cost_estimate=cost(3 << 29, 1 << 22, 1 << 20),
            name="stream",
        )(
            starts,
            queries,
            tokens,
            window,
            far[c][0],
            far[c][1],
            gain_row,
            stream_key,
            stream_value,
            stream_out,
            gain_cross_row,
            *send,
        )
        afters.append(after)

    arrived = lax.all_to_all(send[0], ("slab", "azim"), 0, 0, tiled=True)
    crossed = pl.pallas_call(
        cross_kernel,
        in_specs=[VMEM] * 6,
        out_specs=VMEM,
        out_shape=shape((group, line_count, rows, D), BF16),
        scratch_shapes=[pltpu.VMEM((rows, group * line_count, D), BF16)],
        compiler_params=params(CROSS_MIB),
        cost_estimate=cost(1 << 30, 1 << 21, 1 << 19),
        name="cross",
    )(cross_row, arrived, cross_query, cross_key, cross_value, bias)
    returned = lax.all_to_all(crossed, ("slab", "azim"), 0, 0, tiled=True)

    result = pl.pallas_call(
        final_kernel,
        in_specs=[VMEM] * (2 + CHUNKS),
        out_specs=VMEM,
        out_shape=shape((line_count, length, D), BF16),
        compiler_params=params(FINAL_MIB),
        cost_estimate=cost(1 << 27, 3 << 19),
        name="final",
    )(returned, *afters, cross_out)
    return result.reshape(field.shape)


def solution(mesh):
    in_specs = (
        P("azim", "slab", "stream", None),
        P(),
        P(),
        P(),
        P(),
        P(),
        P(),
        P(),
        P(),
        P(),
        P(),
        P(),
        P(),
        P(),
        P(),
        P("stream", None),
    )
    out_specs = P("azim", "slab", "stream", None)
    return jax.shard_map(
        per_device, mesh=mesh, in_specs=in_specs, out_specs=out_specs, check_vma=False
    )
```

```python
import functools

import jax
import jax.numpy as jnp
from jax import lax
from jax.experimental import pallas as pl
from jax.experimental.pallas import tpu as pltpu
from jax.sharding import PartitionSpec as P

D = 256
HEADS = 4
HEAD_DIM = 64
BLOCK = 128
REACH = 2
LIST_LEN = 4
BLOCKS_DEV = 2
WINDOW = 2 * REACH + 1
LOG2E = 1.4426950408889634
CHUNKS = 2
FETCHED = 7
OWN_MIB = 20
NEAR_MIB = 16
STREAM_MIB = 24
CROSS_MIB = 24
FINAL_MIB = 16
F32 = jnp.float32
BF16 = jnp.bfloat16


def shifted(block, distance):
    size = lax.axis_size("stream")
    return lax.ppermute(block, "stream", [((i - distance) % size, i) for i in range(size)])


def dot(left, right):
    return jnp.dot(left, right, preferred_element_type=F32)


def dot_t(left, right):
    return lax.dot_general(left, right, (((1,), (1,)), ((), ())), preferred_element_type=F32)


def normed_rows(values, gain_row):
    floats = values.astype(F32)
    mean = jnp.mean(floats * floats, axis=-1, keepdims=True)
    return (floats * lax.rsqrt(mean + 1e-05) * gain_row).astype(BF16)


def head_groups():
    rows = lax.broadcasted_iota(jnp.int32, (D, D), 0) // HEAD_DIM
    cols = lax.broadcasted_iota(jnp.int32, (D, D), 1) // HEAD_DIM
    return jnp.where(rows == cols, 1.0 / HEAD_DIM, 0.0).astype(BF16)


def head_units(product, groups):
    means = dot((product * product).astype(BF16), groups)
    return product * lax.rsqrt(means + 1e-06)


def head_stack(queries):
    lane = lax.broadcasted_iota(jnp.int32, queries.shape, 1) // HEAD_DIM
    zero = jnp.zeros_like(queries)
    return jnp.concatenate([jnp.where(lane == h, queries, zero) for h in range(HEADS)], axis=0)


def attend(stack, keys, values):
    weights = jnp.exp2(dot_t(stack, keys))
    factors = 1.0 / jnp.sum(weights, axis=-1, keepdims=True)
    summed = dot(weights.astype(BF16), values)
    count = stack.shape[0] // HEADS
    lane = lax.broadcasted_iota(jnp.int32, (count, D), 1) // HEAD_DIM
    result = summed[:count]
    factor = jnp.broadcast_to(factors[:count], (count, D))
    for h in range(1, HEADS):
        at = slice(h * count, (h + 1) * count)
        result = jnp.where(lane == h, summed[at], result)
        factor = jnp.where(lane == h, factors[at], factor)
    return result * factor


def scale_row(scale_ref):
    head = lax.broadcasted_iota(jnp.int32, (1, D), 1) // HEAD_DIM
    row = jnp.zeros((1, D), F32)
    for h in range(HEADS):
        row = jnp.where(head == h, scale_ref[h] * (LOG2E / HEAD_DIM), row)
    return row


def prepare_kernel(position_ref, *refs, per_azim, size):
    small, fetched, refs = refs[:5], refs[5 : 5 + FETCHED], refs[5 + FETCHED :]
    stream_row_ref, cross_row_ref, start_ref, bias_ref = refs[:4]
    held, refs = refs[4 : 4 + FETCHED], refs[4 + FETCHED :]
    stream_scale_ref, cross_scale_ref, order_ref, table_ref, list_ref, sems = refs
    copies = [
        pltpu.make_async_copy(source, target, sems.at[i])
        for i, (source, target) in enumerate(zip(small + fetched, refs[:5] + held))
    ]
    for copy in copies:
        copy.start()
    for copy in copies[:5]:
        copy.wait()
    stream_row_ref[...] = scale_row(stream_scale_ref)
    cross_row_ref[...] = scale_row(cross_scale_ref)
    for block in range(BLOCKS_DEV):
        for j in range(LIST_LEN):
            named = list_ref[block, j]
            section = lax.rem(named // BLOCKS_DEV + (REACH + size) - position_ref[0], size)
            start_ref[block, j] = section * (BLOCKS_DEV * BLOCK) + (named % BLOCKS_DEV) * BLOCK
    tokens = bias_ref.shape[0]
    azimuths = order_ref.shape[0]

    def placed(axis):
        dims = (tokens, 1) if axis == 0 else (1, HEADS * tokens)
        row = per_azim(lax.broadcasted_iota(jnp.int32, dims, axis) % tokens)
        found = jnp.zeros(dims, jnp.int32)
        for a in range(azimuths):
            found = jnp.where(row == a, order_ref[a], found)
        return found

    distance = placed(0) - placed(1)
    distance = jnp.where(distance < 0, distance + azimuths, distance)
    head = lax.broadcasted_iota(jnp.int32, (1, HEADS * tokens), 1) // tokens
    value = jnp.zeros(bias_ref.shape, F32)
    for m in range(azimuths):
        row = jnp.zeros((1, HEADS * tokens), F32)
        for h in range(HEADS):
            row = jnp.where(head == h, table_ref[h, m] * LOG2E, row)
        value = jnp.where(distance == m, row, value)
    bias_ref[...] = value
    for copy in copies[5:]:
        copy.wait()


def own_kernel(row_ref, field_ref, gain_ref, query_weight_ref, key_weight_ref, value_weight_ref, query_ref, kv_ref):
    lines, length = field_ref.shape[:2]
    groups = head_groups()
    normed = normed_rows(field_ref[...].reshape(-1, D), gain_ref[...])
    keys = head_units(dot(normed, key_weight_ref[...]), groups).astype(BF16)
    kv_ref[:, :, :D] = keys.reshape(lines, length, D)
    queries = head_units(dot(normed, query_weight_ref[...]), groups) * row_ref[...]
    query_ref[...] = queries.astype(BF16).reshape(lines, length, D)
    kv_ref[:, :, D:] = dot(normed, value_weight_ref[...]).astype(BF16).reshape(lines, length, D)


def near_kernel(prev_ref, next_ref, own_ref, gain_ref, key_weight_ref, value_weight_ref, out_ref, *, first_line):
    lines, length = prev_ref.shape[:2]
    groups = head_groups()
    tokens = jnp.concatenate([prev_ref[...].reshape(-1, D), next_ref[...].reshape(-1, D)], axis=0)
    normed = normed_rows(tokens, gain_ref[...])
    keys = head_units(dot(normed, key_weight_ref[...]), groups).astype(BF16)
    values = dot(normed, value_weight_ref[...]).astype(BF16)
    half = lines * length
    for part, place in ((0, 0), (1, 2)):
        at = slice(place * length, (place + 1) * length)
        out_ref[:, at, :D] = keys[part * half : (part + 1) * half].reshape(lines, length, D)
        out_ref[:, at, D:] = values[part * half : (part + 1) * half].reshape(lines, length, D)
    out_ref[:, length : 2 * length] = own_ref[first_line : first_line + lines]


def lines_of(ref):
    return ref.shape[0]


def stream_kernel(
    start_ref,
    query_ref,
    field_ref,
    window_ref,
    far_prev_ref,
    far_next_ref,
    gain_ref,
    key_weight_ref,
    value_weight_ref,
    out_weight_ref,
    gain_cross_ref,
    *refs,
    first_line,
):
    after_ref, send_ref, *far = refs[-2 - lines_of(far_prev_ref) :]
    earlier = refs[: -2 - lines_of(far_prev_ref)]
    lines, length = far_prev_ref.shape[:2]
    groups = head_groups()
    near_rows = window_ref.shape[1]
    group, _, rows, _ = send_ref.shape

    def project(line):
        tokens = jnp.concatenate([far_prev_ref[line], far_next_ref[line]], axis=0).astype(F32)
        gained = (tokens * gain_ref[...]).astype(BF16)
        mean = jnp.mean(tokens * tokens, axis=-1, keepdims=True)
        factor = lax.rsqrt(mean + 1e-05)
        keys = dot(gained, key_weight_ref[...]) * factor
        far[line][:, :D] = head_units(keys, groups).astype(BF16)
        far[line][:, D:] = (dot(gained, value_weight_ref[...]) * factor).astype(BF16)

    def attended(line):
        parts = []
        for block in range(BLOCKS_DEV):
            stack = head_stack(query_ref[first_line + line, block * BLOCK : (block + 1) * BLOCK])
            picked = []
            for j in range(LIST_LEN):
                start = start_ref[block, j]
                before = start < length
                after = start >= length + near_rows
                near_at = jnp.where(before | after, 0, start - length)
                far_at = jnp.where(before, start, jnp.where(after, start - near_rows, 0))
                close = window_ref[line, pl.ds(pl.multiple_of(near_at, BLOCK), BLOCK)]
                distant = far[line][pl.ds(pl.multiple_of(far_at, BLOCK), BLOCK)]
                picked.append(jnp.where(before | after, distant, close))
            listed = jnp.concatenate(picked, axis=0)
            parts.append(attend(stack, listed[:, :D], listed[:, D:]))
        return jnp.concatenate(parts, axis=0).astype(BF16)

    def finish(some, rows_in):
        fields = field_ref[first_line + some.start : first_line + some.stop].reshape(-1, D).astype(F32)
        after = (fields + dot(rows_in, out_weight_ref[...])).astype(BF16)
        after_ref[some] = after.reshape(-1, length, D)
        normed = normed_rows(after, gain_cross_ref[...])
        for line in range(some.start, some.stop):
            at = (line - some.start) * length
            send_ref[:, first_line + line] = normed[at : at + length].reshape(group, rows, D)

    for line in range(lines):
        project(line)
    finish(slice(0, lines), jnp.concatenate([attended(line) for line in range(lines)], axis=0))
    for previous in earlier:
        send_ref[:, :first_line] = previous[:, :first_line]


def turned(block, turn, rows):
    return dot(turn, block.reshape(rows * rows, D)).astype(BF16)


def cross_kernel(
    row_ref,
    source_ref,
    query_weight_ref,
    key_weight_ref,
    value_weight_ref,
    bias_ref,
    out_ref,
    ordered,
):
    groups = head_groups()
    group, line_count, rows = out_ref.shape[:3]
    tokens = group * line_count
    square = rows * rows
    to_row = lax.broadcasted_iota(jnp.int32, (square, square), 0)
    from_row = lax.broadcasted_iota(jnp.int32, (square, square), 1)
    turn = jnp.where(from_row == (to_row % rows) * rows + to_row // rows, 1.0, 0.0).astype(BF16)
    source = source_ref[...].reshape(tokens * rows, D)
    joint = lax.broadcasted_iota(jnp.int32, (HEADS * tokens, D), 0) // tokens
    summing = jnp.where(
        joint == lax.broadcasted_iota(jnp.int32, (HEADS * tokens, D), 1) // HEAD_DIM, 1.0, 0.0
    ).astype(BF16)
    for at in range(0, tokens, rows):
        block = turned(source[at * rows : (at + rows) * rows], turn, rows)
        ordered[:, at : at + rows] = block.reshape(rows, rows, D)
    normed = ordered[...].reshape(rows * tokens, D)
    keys = head_units(dot(normed, key_weight_ref[...]), groups).astype(BF16)
    queries = (head_units(dot(normed, query_weight_ref[...]), groups) * row_ref[...]).astype(BF16)
    values = dot(normed, value_weight_ref[...]).astype(BF16)
    spans = [slice(index * tokens, (index + 1) * tokens) for index in range(rows)]
    weights = []
    for at in spans:
        scores = dot_t(queries[at], head_stack(keys[at])) + bias_ref[...]
        weights.append(jnp.exp2(scores).astype(BF16))
    totals = dot(jnp.concatenate(weights, axis=0), summing)
    summed = jnp.concatenate(
        [dot(part, head_stack(values[at])) for part, at in zip(weights, spans)], axis=0
    )
    ordered[...] = (summed / totals).astype(BF16).reshape(rows, tokens, D)
    lines = rows // line_count
    for at in range(0, tokens, rows):
        block = turned(ordered[:, at : at + rows], turn, rows)
        out_ref[at // line_count : at // line_count + lines] = block.reshape(
            lines, line_count, rows, D
        )


def final_kernel(returned_ref, *refs):
    afters = refs[:CHUNKS]
    weight_ref, out_ref = refs[CHUNKS:]
    line_count, length = out_ref.shape[:2]
    lines = line_count // CHUNKS
    attended = jnp.concatenate(
        [returned_ref[:, line].reshape(-1, D) for line in range(line_count)], axis=0
    )
    after = jnp.concatenate([part[...].reshape(-1, D) for part in afters], axis=0).astype(F32)
    out_ref[...] = (after + dot(attended, weight_ref[...])).astype(BF16).reshape(out_ref.shape)


VMEM = pl.BlockSpec(memory_space=pltpu.VMEM)
SMEM = pl.BlockSpec(memory_space=pltpu.SMEM)


def params(mib):
    return pltpu.CompilerParams(vmem_limit_bytes=mib << 20)


def cost(flops, nbytes, exps=0):
    return pl.CostEstimate(flops=flops, bytes_accessed=nbytes, transcendentals=exps)


def per_device(
    field,
    gain_stream,
    gain_cross,
    stream_query,
    stream_key,
    stream_value,
    stream_out,
    cross_query,
    cross_key,
    cross_value,
    cross_out,
    stream_scale,
    cross_scale,
    azim_bias,
    azim_order,
    block_lists,
):
    line_count = field.shape[0] * field.shape[1]
    length = field.shape[2]
    azims = lax.axis_size("azim")
    slabs = lax.axis_size("slab")
    group = azims * slabs
    rows = length // group
    lines = line_count // CHUNKS
    tokens = field.reshape(line_count, length, D)
    size = lax.axis_size("stream")

    pieces = [tokens[:lines]]
    for c in range(1, CHUNKS):
        held, _ = lax.optimization_barrier((tokens, pieces[-1]))
        pieces.append(held[c * lines : (c + 1) * lines])
    near = [(shifted(piece, 1), shifted(piece, -1)) for piece in pieces]

    gain_row = gain_stream.reshape(1, D)
    gain_cross_row = gain_cross.reshape(1, D)
    lines_per = field.shape[1]
    position = lax.axis_index("stream").astype(jnp.int32).reshape(1)

    def per_azim(token):
        device = token // line_count
        return (device % azims) * field.shape[0] + (token % line_count) // lines_per

    shape = jax.ShapeDtypeStruct
    small = [stream_scale, cross_scale, azim_order, azim_bias, block_lists]
    fetched = [tokens, gain_row, gain_cross_row, stream_query, stream_key, stream_value, stream_out]
    stream_row, cross_row, starts, bias, *held = pl.pallas_call(
        functools.partial(prepare_kernel, per_azim=per_azim, size=size),
        in_specs=[SMEM] + [pl.BlockSpec(memory_space=pltpu.HBM)] * (5 + FETCHED),
        out_specs=[VMEM, VMEM, SMEM, VMEM] + [VMEM] * FETCHED,
        out_shape=[
            shape((1, D), F32),
            shape((1, D), F32),
            shape(block_lists.shape, jnp.int32),
            shape((group * line_count, HEADS * group * line_count), F32),
        ]
        + [shape(array.shape, array.dtype) for array in fetched],
        scratch_shapes=[pltpu.SMEM(array.shape, array.dtype) for array in small]
        + [pltpu.SemaphoreType.DMA((5 + FETCHED,))],
        compiler_params=params(NEAR_MIB),
        cost_estimate=cost(1 << 20, 1 << 18),
        name="prepare",
    )(position, *[pltpu.with_memory_space_constraint(array, pltpu.HBM) for array in small + fetched])
    tokens, gain_row, gain_cross_row, stream_query, stream_key, stream_value, stream_out = held

    far = []
    for c, (ahead, behind) in enumerate(near):
        if c == 0:
            ahead, behind, _ = lax.optimization_barrier((ahead, behind, cross_row))
        far.append((shifted(ahead, 1), shifted(behind, -1)))

    queries, kv_own = pl.pallas_call(
        own_kernel,
        in_specs=[VMEM] * 6,
        out_specs=[VMEM] * 2,
        out_shape=[
            shape((line_count, length, D), BF16),
            shape((line_count, length, 2 * D), BF16),
        ],
        compiler_params=params(OWN_MIB),
        cost_estimate=cost(1 << 29, 1 << 21),
        name="own",
    )(stream_row, tokens, gain_row, stream_query, stream_key, stream_value)

    afters = []
    send = []
    for c in range(CHUNKS):
        window = pl.pallas_call(
            functools.partial(near_kernel, first_line=c * lines),
            in_specs=[VMEM] * 6,
            out_specs=VMEM,
            out_shape=shape((lines, 3 * length, 2 * D), BF16),
            compiler_params=params(NEAR_MIB),
            cost_estimate=cost(1 << 28, 1 << 21),
            name="near",
        )(near[c][0], near[c][1], kv_own, gain_row, stream_key, stream_value)
        after, *send = pl.pallas_call(
            functools.partial(stream_kernel, first_line=c * lines),
            in_specs=[SMEM] + [VMEM] * (10 + len(send)),
            out_specs=[VMEM] * 2,
            out_shape=[shape((lines, length, D), BF16), shape((group, line_count, rows, D), BF16)],
            scratch_shapes=[pltpu.VMEM((2 * length, 2 * D), BF16)] * lines,
            compiler_params=params(STREAM_MIB),
            cost_estimate=cost(3 << 29, 1 << 22, 1 << 20),
            name="stream",
        )(
            starts,
            queries,
            tokens,
            window,
            far[c][0],
            far[c][1],
            gain_row,
            stream_key,
            stream_value,
            stream_out,
            gain_cross_row,
            *send,
        )
        afters.append(after)

    arrived = lax.all_to_all(send[0], ("slab", "azim"), 0, 0, tiled=True)
    crossed = pl.pallas_call(
        cross_kernel,
        in_specs=[VMEM] * 6,
        out_specs=VMEM,
        out_shape=shape((group, line_count, rows, D), BF16),
        scratch_shapes=[pltpu.VMEM((rows, group * line_count, D), BF16)],
        compiler_params=params(CROSS_MIB),
        cost_estimate=cost(1 << 30, 1 << 21, 1 << 19),
        name="cross",
    )(cross_row, arrived, cross_query, cross_key, cross_value, bias)
    returned = lax.all_to_all(crossed, ("slab", "azim"), 0, 0, tiled=True)

    result = pl.pallas_call(
        final_kernel,
        in_specs=[VMEM] * (2 + CHUNKS),
        out_specs=VMEM,
        out_shape=shape((line_count, length, D), BF16),
        compiler_params=params(FINAL_MIB),
        cost_estimate=cost(1 << 27, 3 << 19),
        name="final",
    )(returned, *afters, cross_out)
    return result.reshape(field.shape)


def solution(mesh):
    in_specs = (
        P("azim", "slab", "stream", None),
        P(),
        P(),
        P(),
        P(),
        P(),
        P(),
        P(),
        P(),
        P(),
        P(),
        P(),
        P(),
        P(),
        P(),
        P("stream", None),
    )
    out_specs = P("azim", "slab", "stream", None)
    return jax.shard_map(
        per_device, mesh=mesh, in_specs=in_specs, out_specs=out_specs, check_vma=False
    )
```
